32 devices in a mesh: dp: 16 (over z, y, x), tensor: 2 (over core).
Axes of the slice: x: 2, y: 2, z: 4, core: 2. Of those that a mesh axis runs over, the one named last changes fastest.
Arguments:
- tokens_in: bfloat16 [16384, 1024], P('dp', 'tensor'), may hold values from -6 to 6
- grad_out: bfloat16 [16384, 1024], P('dp', 'tensor'), may hold values from -6 to 6
- doc_len: int32 [64], replicated, may hold values from 1 to 1512, as said below
- doc_pad: int32 [64], replicated, may hold values from 0 to 7, as said below
- doc_owner: int32 [64], replicated, may hold values from 0 to 15, as said below
- doc_perm: int32 [64], replicated, may hold values from 0 to 63, as said below
- w_query: bfloat16 [1024, 2048], P('dp', 'tensor'), may hold values from -0.1875 to 0.1875
- key_matrix: bfloat16 [1024, 1024], P('dp', 'tensor'), may hold values from -0.1875 to 0.1875
- value_matrix: bfloat16 [1024, 1024], P('dp', 'tensor'), may hold values from -0.1875 to 0.1875
- w_output: bfloat16 [2048, 1024], P('tensor', 'dp'), may hold values from -0.5 to 0.5
- w_gate: bfloat16 [1024, 3072], P('dp', 'tensor'), may hold values from -0.1875 to 0.1875
- w_up: bfloat16 [1024, 3072], P('dp', 'tensor'), may hold values from -0.1875 to 0.1875
- w_down: bfloat16 [3072, 1024], P('tensor', 'dp'), may hold values from -0.109375 to 0.109375
- gain_attn: float32 [1024], replicated, may hold values from 0.1 to 1.9
- gain_mlp: float32 [1024], replicated, may hold values from 0.1 to 1.9
- gain_query: float32 [128], replicated, may hold values from 0.1 to 1.9
- gain_key: float32 [128], replicated, may hold values from 0.1 to 1.9
Outputs:
- tokens_out: bfloat16 [16384, 1024], P('dp', 'tensor')
- grad_in: bfloat16 [16384, 1024], P('dp', 'tensor')
- grad_w_query: float32 [1024, 2048], P('dp', 'tensor')
- grad_w_key: float32 [1024, 1024], P('dp', 'tensor')
- grad_w_value: float32 [1024, 1024], P('dp', 'tensor')
- grad_w_output: float32 [2048, 1024], P('tensor', 'dp')
- grad_w_gate: float32 [1024, 3072], P('dp', 'tensor')
- grad_w_up: float32 [1024, 3072], P('dp', 'tensor')
- grad_w_down: float32 [3072, 1024], P('tensor', 'dp')
- grad_gain_attn: float32 [1024], replicated
- grad_gain_mlp: float32 [1024], replicated
- grad_gain_query: float32 [128], replicated
- grad_gain_key: float32 [128], replicated
The draws below stay inside these ranges and needn't reach their ends.
Inputs may be any that keep to these rules, and one draw needn't show every extreme that they name: A document takes (doc_len + doc_pad) / 8 whole tiles. The documents of one owner take between 64 and 192 tiles together, one owner takes exactly 192, and all documents together take 16 * 128 tiles. One document has exactly 1512 real rows. doc_len + doc_pad is a multiple of 8. `doc_owner`: every owner holds exactly 4 documents. `doc_perm`: A permutation of the document ids; the documents of one owner stand next to each other in it.
All inputs are finite; a program needn't handle non-finite values.
Results may differ from the reference program's by a relative error of at most 0.019.
Values may be sent and summed in bfloat16 or wider, within the bound.
No kernel may reach another device: no remote copies, remote signals or barrier semaphores. Data moves between devices by JAX's collectives and lax.ppermute only.
A program may use at most 256 MiB of HBM per device.

```python
import jax
import jax.numpy as jnp
from jax import lax

MODEL_WIDTH = 1024
FF = 3072
QUERY_HEADS = 16
KEY_VALUE_HEADS = 8
HEAD_DIM = 128
TILE = 8
HOME_T = 128
DOCS_DEV = 4
QBLK = 512
CAP_T = 192
LONG_T = 189
TOKENS = 16384
N_DP = 16


def split_counts(weights, totals):
    parts_count = weights.shape[1]
    total_weight = jnp.sum(weights, axis=1, keepdims=True)
    shares = 1 + weights * (totals[:, None] - parts_count) // total_weight
    remainder = totals - jnp.sum(shares[:, :-1], axis=1)
    return jnp.concatenate([shares[:, :-1], remainder[:, None]], axis=1).astype(jnp.int32)


def draw_plan(key):
    base = jax.random.fold_in(key, 4242)
    streams_of_keys = jax.random.split(base, 7)
    pair_order = jax.random.permutation(streams_of_keys[0], N_DP).astype(jnp.int32)
    spread = CAP_T - HOME_T
    shifts = jax.random.randint(streams_of_keys[1], (N_DP // 2,), 0, spread + 1, dtype=jnp.int32)
    shifts = jnp.where(jnp.arange(N_DP // 2) == 0, spread, shifts).astype(jnp.int32)
    paired = jnp.stack([HOME_T + shifts, HOME_T - shifts], axis=1).reshape(N_DP).astype(jnp.int32)
    loads = jnp.zeros((N_DP,), jnp.int32).at[pair_order].set(paired)
    full_owner = pair_order[0]
    weights = jax.random.randint(streams_of_keys[2], (N_DP, DOCS_DEV), 1, 101, dtype=jnp.int32)
    shares = split_counts(weights, loads)
    rest = split_counts(weights[:, 1:], jnp.full((N_DP,), CAP_T - LONG_T, jnp.int32))
    long_shares = jnp.concatenate([jnp.full((N_DP, 1), LONG_T, jnp.int32), rest], axis=1)
    owners = jnp.arange(N_DP, dtype=jnp.int32)
    is_full = (owners == full_owner)[:, None]
    shares = jnp.where(is_full, long_shares, shares)
    pads = jax.random.randint(streams_of_keys[3], (N_DP, DOCS_DEV), 0, TILE, dtype=jnp.int32)
    first_doc = (jnp.arange(DOCS_DEV) == 0)[None, :]
    pads = jnp.where(is_full & first_doc, 0, pads).astype(jnp.int32)
    lengths = (shares * TILE - pads).astype(jnp.int32)
    id_order = jax.random.permutation(streams_of_keys[4], N_DP * DOCS_DEV).astype(jnp.int32)
    slot_of_id = jnp.argsort(id_order).astype(jnp.int32)
    length_by_id = lengths.reshape(-1)[slot_of_id]
    pad_by_id = pads.reshape(-1)[slot_of_id]
    owner_by_id = (slot_of_id // DOCS_DEV).astype(jnp.int32)
    group_order = jax.random.permutation(streams_of_keys[5], N_DP).astype(jnp.int32)
    scores = jax.random.randint(streams_of_keys[6], (N_DP, DOCS_DEV), 0, 1024, dtype=jnp.int32) * DOCS_DEV + jnp.arange(DOCS_DEV, dtype=jnp.int32)[None, :]
    inner = jnp.argsort(scores, axis=1).astype(jnp.int32)
    packed_slots = group_order[:, None] * DOCS_DEV + inner[group_order]
    packed_ids = id_order[packed_slots.reshape(-1)].astype(jnp.int32)
    return (length_by_id, pad_by_id, owner_by_id, packed_ids)


def draw_doc_len(key, part):
    return draw_plan(key)[0]


def draw_doc_pad(key, part):
    return draw_plan(key)[1]


def draw_doc_owner(key, part):
    return draw_plan(key)[2]


def draw_doc_perm(key, part):
    return draw_plan(key)[3]


def steps_of(key, extent, cuts, least, top_value):
    def one(dim, shards_of):
        heights = jax.random.uniform(jax.random.fold_in(jax.random.fold_in(key, 6), dim), (shards_of,), jnp.float32, least / len(cuts), top_value / len(cuts))
        return jnp.repeat(jnp.exp(heights), extent[dim] // shards_of).reshape((-1,) + (1,) * (len(extent) - dim - 1))

    level = one(*cuts[0])
    for cut in cuts[1:]:
        level = level * one(*cut)
    return level


def centred(key, shape, scale, most, cuts=(), kind=jnp.bfloat16):
    values = jax.random.normal(key, shape, jnp.float32) * scale
    if len(cuts) > 0:
        values = steps_of(key, shape, cuts, -0.22, 0.18) * values
    return jnp.clip(values, min=-most, max=most).astype(kind)


def setup_inputs(seed: int = 0) -> dict:
    key_of = jax.random.split(jax.random.key(seed), 18)
    return {
        "tokens_in": centred(key_of[0], (TOKENS, MODEL_WIDTH), 1.0, 6.0, ((0, 16), (1, 2))),
        "grad_out": centred(key_of[1], (TOKENS, MODEL_WIDTH), 1.0, 6.0, ((0, 16), (1, 2))),
        "doc_len": draw_doc_len(jax.random.fold_in(key_of[17], 71), 0),
        "doc_pad": draw_doc_pad(jax.random.fold_in(key_of[17], 71), 0),
        "doc_owner": draw_doc_owner(jax.random.fold_in(key_of[17], 71), 0),
        "doc_perm": draw_doc_perm(jax.random.fold_in(key_of[17], 71), 0),
        "w_query": centred(key_of[6], (MODEL_WIDTH, QUERY_HEADS * HEAD_DIM), MODEL_WIDTH ** -0.5, 0.1875, ((0, 16), (1, 2))),
        "key_matrix": centred(key_of[7], (MODEL_WIDTH, KEY_VALUE_HEADS * HEAD_DIM), MODEL_WIDTH ** -0.5, 0.1875, ((0, 16), (1, 2))),
        "value_matrix": centred(key_of[8], (MODEL_WIDTH, KEY_VALUE_HEADS * HEAD_DIM), MODEL_WIDTH ** -0.5, 0.1875, ((0, 16), (1, 2))),
        "w_output": centred(key_of[9], (QUERY_HEADS * HEAD_DIM, MODEL_WIDTH), (QUERY_HEADS * HEAD_DIM // 16) ** -0.5, 0.5, ((0, 2), (1, 16))),
        "w_gate": centred(key_of[10], (MODEL_WIDTH, FF), MODEL_WIDTH ** -0.5, 0.1875, ((0, 16), (1, 2))),
        "w_up": centred(key_of[11], (MODEL_WIDTH, FF), MODEL_WIDTH ** -0.5, 0.1875, ((0, 16), (1, 2))),
        "w_down": centred(key_of[12], (FF, MODEL_WIDTH), FF ** -0.5, 0.109375, ((0, 2), (1, 16))),
        "gain_attn": jnp.clip(1.0 + 0.18 * jax.random.normal(key_of[13], (MODEL_WIDTH,), jnp.float32), 0.1, 1.9),
        "gain_mlp": jnp.clip(1.0 + 0.18 * jax.random.normal(key_of[14], (MODEL_WIDTH,), jnp.float32), 0.1, 1.9),
        "gain_query": jnp.clip(1.0 + 0.18 * jax.random.normal(key_of[15], (HEAD_DIM,), jnp.float32), 0.1, 1.9),
        "gain_key": jnp.clip(1.0 + 0.18 * jax.random.normal(key_of[16], (HEAD_DIM,), jnp.float32), 0.1, 1.9),
    }


norm_eps = 1e-06
rope_base = 1000000.0
masked_score = -1e+30

@jax.custom_vjp
def reduced_precision(v):
    return lax.optimization_barrier(v.astype(jnp.bfloat16)).astype(jnp.float32)

@jax.custom_vjp
def reduced_backward(v):
    return v

def low_keep(v):
    return (reduced_precision(v), None)

def low_pass(kept, grad):
    return (grad,)

def back_keep(v):
    return (v, None)

def back_low(kept, grad):
    return (reduced_precision(grad),)
reduced_precision.defvjp(low_keep, low_pass)
reduced_backward.defvjp(back_keep, back_low)

def matrix_multiply(left_side, right_side):
    return jnp.dot(left_side, right_side, precision=lax.Precision.HIGHEST, preferred_element_type=jnp.float32)

def layout_tables(doc_len, doc_pad, doc_owner, doc_perm, tile_rows, owner_count):
    doc_count = doc_len.shape[0]
    doc_index = jnp.arange(doc_count, dtype=jnp.int32)
    chosen = doc_perm[:, None] == doc_index[None, :]
    length_packed = lax.optimization_barrier(jnp.sum(jnp.where(chosen, doc_len[None, :], 0), axis=1)).astype(jnp.int32)
    pad_packed = lax.optimization_barrier(jnp.sum(jnp.where(chosen, doc_pad[None, :], 0), axis=1)).astype(jnp.int32)
    owner_packed = lax.optimization_barrier(jnp.sum(jnp.where(chosen, doc_owner[None, :], 0), axis=1)).astype(jnp.int32)
    tiles_packed = ((length_packed + pad_packed) // tile_rows).astype(jnp.int32)
    start_packed = (jnp.cumsum(tiles_packed) - tiles_packed).astype(jnp.int32)
    owners = jnp.arange(owner_count, dtype=jnp.int32)
    member = owner_packed[None, :] == owners[:, None]
    owner_tiles = lax.optimization_barrier(jnp.sum(jnp.where(member, tiles_packed[None, :], 0), axis=1)).astype(jnp.int32)
    owner_start = lax.optimization_barrier(jnp.min(jnp.where(member, start_packed[None, :], 2 ** 30), axis=1)).astype(jnp.int32)
    return (length_packed, tiles_packed, start_packed, owner_packed, owner_tiles, owner_start)

def buffer_rows(owner, tables, cap_tiles, tile_rows):
    length_packed, tiles_packed, start_packed, owner_packed, owner_tiles, owner_start = tables
    owners = jnp.arange(owner_tiles.shape[0], dtype=jnp.int32)
    is_owner = owners == owner
    run_start = jnp.sum(jnp.where(is_owner, owner_start, 0)).astype(jnp.int32)
    run_tiles = jnp.sum(jnp.where(is_owner, owner_tiles, 0)).astype(jnp.int32)
    buffer_tile = jnp.arange(cap_tiles, dtype=jnp.int32)
    packed_tile = run_start + buffer_tile
    inside = buffer_tile < run_tiles
    covers = (packed_tile[:, None] >= start_packed[None, :]) & (packed_tile[:, None] < (start_packed + tiles_packed)[None, :]) & inside[:, None]
    doc_index = jnp.arange(start_packed.shape[0], dtype=jnp.int32)
    doc_of_tile = lax.optimization_barrier(jnp.sum(jnp.where(covers, doc_index[None, :], 0), axis=1)).astype(jnp.int32)
    offset = lax.optimization_barrier(jnp.sum(jnp.where(covers, packed_tile[:, None] - start_packed[None, :], 0), axis=1)).astype(jnp.int32)
    length = lax.optimization_barrier(jnp.sum(jnp.where(covers, length_packed[None, :], 0), axis=1)).astype(jnp.int32)
    within = jnp.arange(tile_rows, dtype=jnp.int32)
    position_grid = offset[:, None] * tile_rows + within[None, :]
    doc_key = jnp.broadcast_to(jnp.where(inside, doc_of_tile, -1)[:, None], (cap_tiles, tile_rows)).reshape(-1)
    valid = (inside[:, None] & (position_grid < length[:, None])).reshape(-1)
    return (doc_key, position_grid.reshape(-1).astype(jnp.int32), valid)

def allowed_block(doc_key, position, valid, begin, block_rows):
    rows_query = begin + jnp.arange(block_rows, dtype=jnp.int32)
    key_query = lax.dynamic_slice_in_dim(doc_key, begin, block_rows, 0)
    position_query = lax.dynamic_slice_in_dim(position, begin, block_rows, 0)
    valid_query = lax.dynamic_slice_in_dim(valid, begin, block_rows, 0)
    key_rows = jnp.arange(doc_key.shape[0], dtype=jnp.int32)
    same = (key_query[:, None] == doc_key[None, :]) & (position[None, :] <= position_query[:, None]) & valid_query[:, None] & valid[None, :]
    return same | (rows_query[:, None] == key_rows[None, :])

def rope_tables(position, head_size):
    exponent = jnp.arange(head_size // 2, dtype=jnp.float32) * (2.0 / head_size)
    frequency = rope_base ** (-exponent)
    angle = position.astype(jnp.float32)[:, None] * frequency[None, :]
    return (jnp.cos(angle), jnp.sin(angle))

def rotate(values, cosine, sine):
    half_size = values.shape[-1] // 2
    front_half = values[..., :half_size]
    back_half = values[..., half_size:]
    cosine_wide = cosine[:, None, :]
    sine_wide = sine[:, None, :]
    return jnp.concatenate([front_half * cosine_wide - back_half * sine_wide, back_half * cosine_wide + front_half * sine_wide], axis=-1)

def head_norm(values, gain):
    return values * lax.rsqrt(lax.optimization_barrier(jnp.mean(values * values, axis=-1, keepdims=True)) + norm_eps) * gain

def owner_layer(rows_in, doc_key, position, valid, params):
    w_query, key_matrix, value_matrix, w_output, w_gate, w_up, w_down, gain_attn, gain_mlp, gain_query, gain_key = params
    count_of_rows = rows_in.shape[0]
    head_group = QUERY_HEADS // KEY_VALUE_HEADS
    scale = HEAD_DIM ** (-0.5)
    inv_first = lax.rsqrt(lax.optimization_barrier(jnp.mean(rows_in * rows_in, axis=-1, keepdims=True)) + norm_eps)
    attention_normed = reduced_precision(rows_in * inv_first * gain_attn)
    queries = reduced_backward(matrix_multiply(attention_normed, w_query)).reshape(count_of_rows, QUERY_HEADS, HEAD_DIM)
    unrotated_keys = reduced_backward(matrix_multiply(attention_normed, key_matrix)).reshape(count_of_rows, KEY_VALUE_HEADS, HEAD_DIM)
    reduced_values = reduced_precision(reduced_backward(matrix_multiply(attention_normed, value_matrix))).reshape(count_of_rows, KEY_VALUE_HEADS, HEAD_DIM)
    cosine, sine = rope_tables(position, HEAD_DIM)
    query_low = reduced_precision(rotate(head_norm(queries, gain_query), cosine, sine))
    key_low = reduced_precision(rotate(head_norm(unrotated_keys, gain_key), cosine, sine))
    key_wide = jnp.repeat(key_low, head_group, axis=1)
    value_wide = jnp.repeat(reduced_values, head_group, axis=1)

    def attend(index):
        begin = index * QBLK
        query_block = lax.dynamic_slice_in_dim(query_low, begin, QBLK, 0)
        scores = reduced_backward(jnp.einsum('qhd,khd->hqk', query_block, key_wide, precision=lax.Precision.HIGHEST) * scale)
        allowed = allowed_block(doc_key, position, valid, begin, QBLK)
        masked = jnp.where(allowed[None], scores, masked_score)
        top = lax.optimization_barrier(jnp.max(masked, axis=-1, keepdims=True))
        expo = jnp.exp(masked - top)
        prob = reduced_precision(expo / lax.optimization_barrier(jnp.sum(expo, axis=-1, keepdims=True)))
        return jnp.einsum('hqk,khd->qhd', prob, value_wide, precision=lax.Precision.HIGHEST)
    attended = lax.map(jax.checkpoint(attend), jnp.arange(count_of_rows // QBLK, dtype=jnp.int32))
    attended = reduced_precision(reduced_backward(attended.reshape(count_of_rows, QUERY_HEADS * HEAD_DIM)))
    middle = rows_in + reduced_backward(matrix_multiply(attended, w_output))
    inv_second = lax.rsqrt(lax.optimization_barrier(jnp.mean(middle * middle, axis=-1, keepdims=True)) + norm_eps)
    normed_second = reduced_precision(middle * inv_second * gain_mlp)
    gate = reduced_backward(matrix_multiply(normed_second, w_gate))
    up_part = reduced_backward(matrix_multiply(normed_second, w_up))
    activated = reduced_precision(jax.nn.silu(gate) * up_part)
    return middle + reduced_backward(matrix_multiply(activated, w_down))

def reference(tokens_in, grad_out, doc_len, doc_pad, doc_owner, doc_perm, w_query, key_matrix, value_matrix, w_output, w_gate, w_up, w_down, gain_attn, gain_mlp, gain_query, gain_key):
    tables = layout_tables(doc_len, doc_pad, doc_owner, doc_perm, TILE, N_DP)
    owner_tiles = tables[4]
    owner_start = tables[5]
    owners = jnp.arange(N_DP, dtype=jnp.int32)

    def rows_of(owner):
        return buffer_rows(owner, tables, CAP_T, TILE)
    doc_key, position, valid = jax.vmap(rows_of)(owners)
    buffer_tile = jnp.arange(CAP_T, dtype=jnp.int32)
    packed_tile = owner_start[:, None] + buffer_tile[None, :]
    inside = buffer_tile[None, :] < owner_tiles[:, None]
    home_index = packed_tile % N_DP * HOME_T + packed_tile // N_DP
    gather_index = jnp.where(inside, home_index, N_DP * HOME_T).reshape(-1).astype(jnp.int32)
    home_tile = jnp.arange(N_DP * HOME_T, dtype=jnp.int32)
    packed_of_home = home_tile % HOME_T * N_DP + home_tile // HOME_T
    owned = (packed_of_home[:, None] >= owner_start[None, :]) & (packed_of_home[:, None] < (owner_start + owner_tiles)[None, :])
    owner_of = lax.optimization_barrier(jnp.sum(jnp.where(owned, owners[None, :], 0), axis=1)).astype(jnp.int32)
    start_of = lax.optimization_barrier(jnp.sum(jnp.where(owned, owner_start[None, :], 0), axis=1)).astype(jnp.int32)
    back_index = (owner_of * CAP_T + packed_of_home - start_of).astype(jnp.int32)

    def to_owner(home_rows):
        tiles = home_rows.reshape(N_DP * HOME_T, TILE, home_rows.shape[1])
        tiles = jnp.concatenate([tiles, jnp.zeros((1, TILE, home_rows.shape[1]), tiles.dtype)], axis=0)
        return jnp.take(tiles, gather_index, axis=0).reshape(N_DP, CAP_T * TILE, home_rows.shape[1])

    def to_home(owner_rows):
        tiles = owner_rows.reshape(N_DP * CAP_T, TILE, owner_rows.shape[2])
        return jnp.take(tiles, back_index, axis=0).reshape(TOKENS, owner_rows.shape[2])
    params = (w_query.astype(jnp.float32), key_matrix.astype(jnp.float32), value_matrix.astype(jnp.float32), w_output.astype(jnp.float32), w_gate.astype(jnp.float32), w_up.astype(jnp.float32), w_down.astype(jnp.float32), gain_attn.astype(jnp.float32), gain_mlp.astype(jnp.float32), gain_query.astype(jnp.float32), gain_key.astype(jnp.float32))

    def forward(tokens, weights):
        buffers = to_owner(tokens)

        def per_owner(carry, items):
            rows_in, keys_doc, positions, valids = items
            return (carry, owner_layer(rows_in, keys_doc, positions, valids, weights))
        final_carry, outputs = lax.scan(jax.checkpoint(per_owner), jnp.zeros((), jnp.float32), (buffers, doc_key, position, valid))
        return outputs
    outputs, pullback = jax.vjp(forward, tokens_in.astype(jnp.float32), params)
    cotangent = jnp.where(valid[:, :, None], to_owner(grad_out.astype(jnp.float32)), 0.0)
    grad_tokens, grad_params = pullback(cotangent)
    tokens_out = to_home(outputs).astype(jnp.bfloat16)
    grad_in = grad_tokens.astype(jnp.bfloat16)
    return (tokens_out, grad_in, grad_params[0], grad_params[1], grad_params[2], grad_params[3], grad_params[4], grad_params[5], grad_params[6], grad_params[7], grad_params[8], grad_params[9], grad_params[10])
```

```python
import functools
import math

import jax
import jax.numpy as jnp
from jax import lax
from jax.experimental import pallas as pl
from jax.experimental.pallas import tpu as pltpu
from jax.sharding import PartitionSpec as P

HEAD_DIM = 128
TILE = 8
CAP_T = 192
ROWS = 256
BLK = 256
GROUP = 2

norm_eps = 1e-06
rope_base = 1000000.0


bf16 = jnp.bfloat16
f32 = jnp.float32


def dot(a, b, da, db):
    return lax.dot_general(a, b, (((da,), (db,)), ((), ())), preferred_element_type=f32)


def layout_tables(doc_len, doc_pad, doc_owner, doc_perm, tile_rows, owner_count):
    doc_count = doc_len.shape[0]
    doc_index = jnp.arange(doc_count, dtype=jnp.int32)
    chosen = doc_perm[:, None] == doc_index[None, :]
    length_packed = jnp.sum(jnp.where(chosen, doc_len[None, :], 0), axis=1)
    pad_packed = jnp.sum(jnp.where(chosen, doc_pad[None, :], 0), axis=1)
    owner_packed = jnp.sum(jnp.where(chosen, doc_owner[None, :], 0), axis=1)
    tiles_packed = (length_packed + pad_packed) // tile_rows
    start_packed = jnp.cumsum(tiles_packed) - tiles_packed
    owners = jnp.arange(owner_count, dtype=jnp.int32)
    member = owner_packed[None, :] == owners[:, None]
    owner_tiles = jnp.sum(jnp.where(member, tiles_packed[None, :], 0), axis=1)
    owner_start = jnp.min(jnp.where(member, start_packed[None, :], 2**30), axis=1)
    return (length_packed, tiles_packed, start_packed, owner_packed, owner_tiles, owner_start)


def buffer_rows(owner, tables, cap_tiles, tile_rows):
    length_packed, tiles_packed, start_packed, owner_packed, owner_tiles, owner_start = tables
    owners = jnp.arange(owner_tiles.shape[0], dtype=jnp.int32)
    is_owner = owners == owner
    run_start = jnp.sum(jnp.where(is_owner, owner_start, 0))
    run_tiles = jnp.sum(jnp.where(is_owner, owner_tiles, 0))
    buffer_tile = jnp.arange(cap_tiles, dtype=jnp.int32)
    packed_tile = run_start + buffer_tile
    inside = buffer_tile < run_tiles
    covers = (
        (packed_tile[:, None] >= start_packed[None, :])
        & (packed_tile[:, None] < (start_packed + tiles_packed)[None, :])
        & inside[:, None]
    )
    offset = jnp.sum(jnp.where(covers, packed_tile[:, None] - start_packed[None, :], 0), axis=1)
    length = jnp.sum(jnp.where(covers, length_packed[None, :], 0), axis=1)
    within = jnp.arange(tile_rows, dtype=jnp.int32)
    position_grid = offset[:, None] * tile_rows + within[None, :]
    valid = (inside[:, None] & (position_grid < length[:, None])).reshape(-1)
    return (position_grid.reshape(-1), valid)


def rope_tables(position, head_size):
    exponent = jnp.arange(head_size // 2, dtype=f32) * (2.0 / head_size)
    frequency = rope_base ** (-exponent)
    angle = position.astype(f32)[:, None] * frequency[None, :]
    cosine, sine = jnp.cos(angle), jnp.sin(angle)
    return (
        jnp.concatenate([cosine, cosine], axis=1),
        jnp.concatenate([-sine, sine], axis=1),
    )


def swap_halves(v):
    return pltpu.roll(v, HEAD_DIM // 2, 1)


def qkv_kernel(x_ref, w0_ref, w1_ref, gain_ref, gq_ref, gk_ref, cos_ref, sin_ref,
               n_ref, q_ref, k_ref, v_ref, raw_ref):
    x = x_ref[...].astype(f32)
    inv = lax.rsqrt(jnp.mean(x * x, axis=-1, keepdims=True) + norm_eps)
    normed = (x * inv * gain_ref[...]).astype(bf16)
    n_ref[...] = normed
    cosine = cos_ref[...]
    sine = sin_ref[...]
    nq = q_ref.shape[1]
    nk = k_ref.shape[1]

    def heads(raw, gain, out_ref):
        for h in range(raw.shape[1] // HEAD_DIM):
            one = raw[:, h * HEAD_DIM:(h + 1) * HEAD_DIM]
            hinv = lax.rsqrt(jnp.mean(one * one, axis=-1, keepdims=True) + norm_eps)
            g = one * hinv * gain
            out_ref[:, h * HEAD_DIM:(h + 1) * HEAD_DIM] = (
                g * cosine + swap_halves(g) * sine
            ).astype(bf16)

    raw_q = dot(normed, w0_ref[...], 1, 0)
    raw_ref[:, :nq] = raw_q
    heads(raw_q, gq_ref[...], q_ref)
    raw_kv = dot(normed, w1_ref[...], 1, 0)
    raw_ref[:, nq:] = raw_kv[:, :nk]
    heads(raw_kv[:, :nk], gk_ref[...], k_ref)
    v_ref[...] = raw_kv[:, nk:].astype(bf16)


def row_spec(cols, rows=ROWS):
    return pl.BlockSpec((rows, cols), lambda i: (i, 0))


def full_spec(a):
    return pl.BlockSpec(a.shape, lambda i: (0,) * a.ndim, pipeline_mode=pl.Buffered(1))


def qkv_call(x, w0, w1, gain, gq, gk, cosine, sine):
    rows, width = x.shape
    nq, nkv = w0.shape[1], w1.shape[1]
    nk = nkv // 2
    shape = jax.ShapeDtypeStruct
    return pl.pallas_call(
        qkv_kernel,
        grid=(rows // ROWS,),
        in_specs=[row_spec(width), full_spec(w0), full_spec(w1), full_spec(gain), full_spec(gq),
                  full_spec(gk), row_spec(HEAD_DIM), row_spec(HEAD_DIM)],
        out_specs=[row_spec(width), row_spec(nq), row_spec(nk), row_spec(nk), row_spec(nq + nk)],
        out_shape=[shape((rows, width), bf16), shape((rows, nq), bf16), shape((rows, nk), bf16),
                   shape((rows, nk), bf16), shape((rows, nq + nk), f32)],
        name="qkv",
        cost_estimate=pl.CostEstimate(flops=2 * rows * width * (nq + nkv), transcendentals=0,
                                      bytes_accessed=rows * (nq + nkv) * 8),
    )(x, w0, w1, gain, gq, gk, cosine, sine)


SCORE_EXP2 = HEAD_DIM ** (-0.5) * math.log2(math.e)


def attend_kernel(lo_ref, hm_ref, q_ref, k_ref, v_ref, start_ref, o_ref, il_ref, acc_ref):
    i = pl.program_id(1)
    acc_ref[...] = jnp.zeros_like(acc_ref)
    row = i * BLK + lax.broadcasted_iota(jnp.int32, (BLK, BLK), 0)
    col0 = lax.broadcasted_iota(jnp.int32, (BLK, BLK), 1)
    ones = jnp.ones((BLK, HEAD_DIM), bf16)

    def step(j, masked):
        at = pl.multiple_of(j * BLK, BLK)
        k = k_ref[pl.ds(at, BLK), :]
        v = jnp.concatenate([v_ref[pl.ds(at, BLK), :], ones], axis=1)
        if masked:
            col = col0 + j * BLK
            allowed = (col >= start_ref[...]) & (col <= row)
        for g in range(GROUP):
            s = dot(q_ref[:, g * HEAD_DIM:(g + 1) * HEAD_DIM], k, 1, 1)
            p = jnp.exp2(s * SCORE_EXP2)
            if masked:
                p = jnp.where(allowed, p, 0.0)
            acc_ref[g] += dot(p.astype(bf16), v, 1, 0)

    lo = lo_ref[i]
    hm = hm_ref[i]
    pl.loop(lo, hm)(lambda j: step(j, True))
    pl.loop(hm, i)(lambda j: step(j, False))
    step(i, True)
    for g in range(GROUP):
        total = acc_ref[g, :, HEAD_DIM:]
        inv = 1.0 / total
        o_ref[:, g * HEAD_DIM:(g + 1) * HEAD_DIM] = (acc_ref[g, :, :HEAD_DIM] * inv).astype(bf16)
        il_ref[0, g:g + 1, :] = jnp.transpose(inv)[0:1, :]


def attend_call(lo, hm, q, k, v, start, first, count):
    rows = q.shape[0]
    nb = rows // BLK
    wide = GROUP * HEAD_DIM
    shape = jax.ShapeDtypeStruct
    return pl.pallas_call(
        attend_kernel,
        grid_spec=pltpu.PrefetchScalarGridSpec(
            num_scalar_prefetch=2,
            grid=(count, nb),
            in_specs=[
                pl.BlockSpec((BLK, wide), lambda h, i, lo, hm: (i, h + first)),
                pl.BlockSpec((rows, HEAD_DIM), lambda h, i, lo, hm: (0, h + first)),
                pl.BlockSpec((rows, HEAD_DIM), lambda h, i, lo, hm: (0, h + first)),
                pl.BlockSpec((BLK, 1), lambda h, i, lo, hm: (i, 0)),
            ],
            out_specs=[
                pl.BlockSpec((BLK, wide), lambda h, i, lo, hm: (i, h)),
                pl.BlockSpec((1, 8, BLK), lambda h, i, lo, hm: (h, 0, i)),
            ],
            scratch_shapes=[pltpu.VMEM((GROUP, BLK, wide), f32)],
        ),
        out_shape=[shape((rows, count * wide), bf16), shape((count, 8, rows), f32)],
        name="attend",
        cost_estimate=pl.CostEstimate(flops=4 * rows * rows * count * wide, transcendentals=0,
                                      bytes_accessed=rows * count * wide * 8),
    )(lo, hm, q, k, v, start)


def back_heads(dx, raw, cosine, sine, gain):
    dn = dx * cosine - swap_halves(dx) * sine
    hinv = lax.rsqrt(jnp.mean(raw * raw, axis=-1, keepdims=True) + norm_eps)
    hat = raw * hinv
    scaled = dn * gain
    out = hinv * (scaled - hat * jnp.mean(scaled * hat, axis=-1, keepdims=True))
    return out.astype(bf16), jnp.sum(dn * hat, axis=0, keepdims=True)


def attend_back_kernel(lo_ref, hm_ref, q_ref, k_ref, v_ref, o_ref, do_ref, il_ref, start_ref,
                       rawq_ref, rawk_ref, cos_ref, sin_ref, gq_ref, gk_ref,
                       dq_ref, dk_ref, dv_ref, gain_ref, dk_acc, dv_acc, dq_acc):
    h = pl.program_id(0)
    i = pl.program_id(1)
    last = pl.num_programs(1) - 1

    @pl.when((h == 0) & (i == 0))
    def _():
        gain_ref[...] = jnp.zeros_like(gain_ref)

    @pl.when(i == 0)
    def _():
        dk_acc[...] = jnp.zeros_like(dk_acc)
        dv_acc[...] = jnp.zeros_like(dv_acc)

    dq_acc[...] = jnp.zeros_like(dq_acc)
    row = i * BLK + lax.broadcasted_iota(jnp.int32, (BLK, BLK), 1)
    col0 = lax.broadcasted_iota(jnp.int32, (BLK, BLK), 0)
    start = start_ref[...]
    deltas = []
    for g in range(GROUP):
        lanes = slice(g * HEAD_DIM, (g + 1) * HEAD_DIM)
        prod = do_ref[:, lanes].astype(f32) * o_ref[:, lanes].astype(f32)
        deltas.append(jnp.sum(jnp.transpose(prod), axis=0, keepdims=True))

    def step(j, masked):
        at = pl.multiple_of(j * BLK, BLK)
        k = k_ref[pl.ds(at, BLK), :]
        v = v_ref[pl.ds(at, BLK), :]
        if masked:
            col = col0 + j * BLK
            allowed = (col >= start) & (col <= row)
        dk = []
        dv = []
        for g in range(GROUP):
            lanes = slice(g * HEAD_DIM, (g + 1) * HEAD_DIM)
            q = q_ref[:, lanes]
            do = do_ref[:, lanes]
            s = dot(k, q, 1, 1)
            p = jnp.exp2(s * SCORE_EXP2) * il_ref[0, g:g + 1, :]
            if masked:
                p = jnp.where(allowed, p, 0.0)
            dp = dot(v, do, 1, 1)
            ds = (p * (dp - deltas[g])).astype(bf16)
            dv.append(dot(p.astype(bf16), do, 1, 0))
            dk.append(dot(ds, q, 1, 0))
            dq_acc[:, lanes] += dot(ds, k, 0, 0)
        dk_acc[pl.ds(at, BLK), :] += dk[0] + dk[1]
        dv_acc[pl.ds(at, BLK), :] += dv[0] + dv[1]

    lo = lo_ref[i]
    hm = hm_ref[i]
    pl.loop(lo, hm)(lambda j: step(j, True))
    pl.loop(hm, i)(lambda j: step(j, False))
    step(i, True)
    scale = HEAD_DIM ** (-0.5)
    rows = pl.ds(pl.multiple_of(i * BLK, BLK), BLK)
    for g in range(GROUP):
        lanes = slice(g * HEAD_DIM, (g + 1) * HEAD_DIM)
        out, part = back_heads(dq_acc[:, lanes] * scale, rawq_ref[:, lanes], cos_ref[rows, :],
                               sin_ref[rows, :], gq_ref[...])
        dq_ref[:, lanes] = out
        gain_ref[0:1, :] += part

    @pl.when(i == last)
    def _():
        @pl.loop(0, last + 1)
        def _(j):
            rr = pl.ds(pl.multiple_of(j * BLK, BLK), BLK)
            out, part = back_heads(dk_acc[rr, :] * scale, rawk_ref[rr, :], cos_ref[rr, :],
                                   sin_ref[rr, :], gk_ref[...])
            dk_ref[rr, :] = out
            gain_ref[1:2, :] += part
            dv_ref[rr, :] = dv_acc[rr, :].astype(bf16)


def attend_back_call(lo, hm, q, k, v, o, do, il, start, raw, cosine, sine, gq, gk, first, count):
    rows = q.shape[0]
    nb = rows // BLK
    wide = GROUP * HEAD_DIM
    raw_k0 = q.shape[1] // HEAD_DIM
    shape = jax.ShapeDtypeStruct
    whole = pl.BlockSpec((rows, HEAD_DIM), lambda h, i, lo, hm: (0, h + first))
    table = pl.BlockSpec((rows, HEAD_DIM), lambda h, i, lo, hm: (0, 0))
    gain = pl.BlockSpec((1, HEAD_DIM), lambda h, i, lo, hm: (0, 0))
    local = pl.BlockSpec((BLK, wide), lambda h, i, lo, hm: (i, h))
    shifted = pl.BlockSpec((BLK, wide), lambda h, i, lo, hm: (i, h + first))
    return pl.pallas_call(
        attend_back_kernel,
        grid_spec=pltpu.PrefetchScalarGridSpec(
            num_scalar_prefetch=2,
            grid=(count, nb),
            in_specs=[
                shifted, whole, whole, local, local,
                pl.BlockSpec((1, 8, BLK), lambda h, i, lo, hm: (h, 0, i)),
                pl.BlockSpec((1, BLK), lambda h, i, lo, hm: (0, i)),
                shifted,
                pl.BlockSpec((rows, HEAD_DIM), lambda h, i, lo, hm: (0, raw_k0 + h + first)),
                table, table, gain, gain,
            ],
            out_specs=[
                local,
                pl.BlockSpec((rows, HEAD_DIM), lambda h, i, lo, hm: (0, h)),
                pl.BlockSpec((rows, HEAD_DIM), lambda h, i, lo, hm: (0, h)),
                pl.BlockSpec((8, HEAD_DIM), lambda h, i, lo, hm: (0, 0)),
            ],
            scratch_shapes=[
                pltpu.VMEM((rows, HEAD_DIM), f32),
                pltpu.VMEM((rows, HEAD_DIM), f32),
                pltpu.VMEM((BLK, wide), f32),
            ],
        ),
        out_shape=[shape((rows, count * wide), bf16), shape((rows, count * HEAD_DIM), bf16),
                   shape((rows, count * HEAD_DIM), bf16), shape((8, HEAD_DIM), f32)],
        name="attend_back",
        cost_estimate=pl.CostEstimate(flops=10 * rows * rows * count * wide, transcendentals=0,
                                      bytes_accessed=rows * count * wide * 16),
    )(lo, hm, q, k, v, o, do, il, start, raw, raw, cosine, sine, gq, gk)


def mlp_kernel(x_ref, a_ref, b_ref, gain_ref, wg_ref, wu_ref, d0_ref, d1_ref,
               mid_ref, n_ref, gate_ref, up_ref, a0_ref, a1_ref, br_ref):
    mid = x_ref[...].astype(f32) + (a_ref[...].astype(f32) + b_ref[...].astype(f32))
    mid_ref[...] = mid
    inv = lax.rsqrt(jnp.mean(mid * mid, axis=-1, keepdims=True) + norm_eps)
    normed = (mid * inv * gain_ref[...]).astype(bf16)
    n_ref[...] = normed
    gate = dot(normed, wg_ref[...], 1, 0)
    up = dot(normed, wu_ref[...], 1, 0)
    gate_ref[...] = gate
    up_ref[...] = up
    act = (gate * jax.nn.sigmoid(gate) * up).astype(bf16)
    half = a0_ref.shape[1]
    a0_ref[...] = act[:, :half]
    a1_ref[...] = act[:, half:]
    br_ref[...] = (dot(act[:, :half], d0_ref[...], 1, 1)
                   + dot(act[:, half:], d1_ref[...], 1, 1)).astype(bf16)


def mlp_call(x, a, b, gain, wg, wu, d0, d1):
    rows, width = x.shape
    ff = wg.shape[1]
    shape = jax.ShapeDtypeStruct
    return pl.pallas_call(
        mlp_kernel,
        grid=(rows // ROWS,),
        in_specs=[row_spec(width)] * 3 + [full_spec(t) for t in (gain, wg, wu, d0, d1)],
        out_specs=[row_spec(width), row_spec(width), row_spec(ff), row_spec(ff),
                   row_spec(ff // 2), row_spec(ff // 2), row_spec(width)],
        out_shape=[shape((rows, width), f32), shape((rows, width), bf16), shape((rows, ff), f32),
                   shape((rows, ff), f32), shape((rows, ff // 2), bf16),
                   shape((rows, ff // 2), bf16), shape((rows, width), bf16)],
        name="mlp",
        cost_estimate=pl.CostEstimate(flops=6 * rows * width * ff, transcendentals=0,
                                      bytes_accessed=rows * ff * 14),
    )(x, a, b, gain, wg, wu, d0, d1)


def mlp_back_kernel(cot_ref, mid_ref, gate_ref, up_ref, gain_ref, wg_ref, wu_ref, d0_ref, d1_ref,
                    dg_ref, du_ref, part_ref, acc_ref):
    cot = cot_ref[...]
    half = d0_ref.shape[1]
    for s, d_ref in ((slice(0, half), d0_ref), (slice(half, 2 * half), d1_ref)):
        d_act = dot(cot, d_ref[...], 1, 0)
        gate = gate_ref[:, s]
        sig = jax.nn.sigmoid(gate)
        dg_ref[:, s] = (d_act * up_ref[:, s] * (sig * (1.0 + gate * (1.0 - sig)))).astype(bf16)
        du_ref[:, s] = (d_act * (gate * sig)).astype(bf16)
    dn = dot(dg_ref[...], wg_ref[...], 1, 1) + dot(du_ref[...], wu_ref[...], 1, 1)
    mid = mid_ref[...]
    inv = lax.rsqrt(jnp.mean(mid * mid, axis=-1, keepdims=True) + norm_eps)
    hat = mid * inv
    scaled = dn * gain_ref[...]
    part_ref[...] = (inv * (scaled - hat * jnp.mean(scaled * hat, axis=-1, keepdims=True))).astype(bf16)

    @pl.when(pl.program_id(0) == 0)
    def _():
        acc_ref[...] = jnp.zeros_like(acc_ref)

    acc_ref[...] += jnp.sum(dn * hat, axis=0, keepdims=True)


def mlp_back_call(cot, mid, gate, up, gain, wg, wu, d0, d1):
    rows, width = mid.shape
    ff = wg.shape[1]
    shape = jax.ShapeDtypeStruct
    return pl.pallas_call(
        mlp_back_kernel,
        grid=(rows // ROWS,),
        in_specs=[row_spec(width), row_spec(width), row_spec(ff), row_spec(ff)]
        + [full_spec(t) for t in (gain, wg, wu, d0, d1)],
        out_specs=[row_spec(ff), row_spec(ff), row_spec(width),
                   pl.BlockSpec((1, width), lambda i: (0, 0))],
        out_shape=[shape((rows, ff), bf16), shape((rows, ff), bf16), shape((rows, width), bf16),
                   shape((1, width), f32)],
        name="mlp_back",
        cost_estimate=pl.CostEstimate(flops=6 * rows * width * ff, transcendentals=0,
                                      bytes_accessed=rows * ff * 12),
    )(cot, mid, gate, up, gain, wg, wu, d0, d1)


def in_back_kernel(q0_ref, q1_ref, k0_ref, k1_ref, v0_ref, v1_ref, x_ref, gain_ref, w0_ref, w1_ref,
                   part_ref, acc_ref):
    hq = q0_ref.shape[1]
    hk = k0_ref.shape[1]
    nk = 2 * hk
    dn = (
        dot(q0_ref[...], w0_ref[:, :hq], 1, 1)
        + dot(q1_ref[...], w0_ref[:, hq:], 1, 1)
        + dot(k0_ref[...], w1_ref[:, :hk], 1, 1)
        + dot(k1_ref[...], w1_ref[:, hk:nk], 1, 1)
        + dot(v0_ref[...], w1_ref[:, nk:nk + hk], 1, 1)
        + dot(v1_ref[...], w1_ref[:, nk + hk:], 1, 1)
    )
    x = x_ref[...].astype(f32)
    inv = lax.rsqrt(jnp.mean(x * x, axis=-1, keepdims=True) + norm_eps)
    hat = x * inv
    scaled = dn * gain_ref[...]
    part_ref[...] = (inv * (scaled - hat * jnp.mean(scaled * hat, axis=-1, keepdims=True))).astype(bf16)

    @pl.when(pl.program_id(0) == 0)
    def _():
        acc_ref[...] = jnp.zeros_like(acc_ref)

    acc_ref[...] += jnp.sum(dn * hat, axis=0, keepdims=True)


def in_back_call(q0, q1, k0, k1, v0, v1, x, gain, w0, w1):
    rows, width = x.shape
    shape = jax.ShapeDtypeStruct
    return pl.pallas_call(
        in_back_kernel,
        grid=(rows // ROWS,),
        in_specs=[row_spec(t.shape[1]) for t in (q0, q1, k0, k1, v0, v1, x)]
        + [full_spec(t) for t in (gain, w0, w1)],
        out_specs=[row_spec(width), pl.BlockSpec((1, width), lambda i: (0, 0))],
        out_shape=[shape((rows, width), bf16), shape((1, width), f32)],
        name="in_back",
        cost_estimate=pl.CostEstimate(flops=2 * rows * width * (w0.shape[1] + w1.shape[1]),
                                      transcendentals=0, bytes_accessed=rows * width * 8),
    )(q0, q1, k0, k1, v0, v1, x, gain, w0, w1)


def factors_of(count):
    if count == 64:
        return (4, 2, 4, 2)
    out = []
    if count % 4 == 0:
        out.append(4)
        count //= 4
    while count > 1:
        f = next(p for p in range(2, count + 1) if count % p == 0)
        out.append(f)
        count //= f
    return tuple(out)


class Moves:
    def __init__(self, count, index):
        self.factors = factors_of(count)
        self.count = count
        strides = []
        s = count
        for f in self.factors:
            s //= f
            strides.append(s)
        self.strides = strides
        self.digits = [(index // st) % f for st, f in zip(strides, self.factors)]

    def orders(self):
        n = len(self.factors)
        return (tuple(range(n)), (0,) + tuple(reversed(range(1, n))))

    def shift(self, value, axis, step):
        f, st = self.factors[axis], self.strides[axis]
        pairs = []
        for i in range(self.count):
            d = (i // st) % f
            pairs.append((i, i + (((d + step) % f) - d) * st))
        return lax.ppermute(value, "dp", pairs)

    def gather(self, shard, color):
        cur = shard[None]
        done = []
        for axis in self.orders()[color]:
            f = self.factors[axis]
            digit = self.digits[axis]
            got = [cur] + [self.shift(cur, axis, s) for s in range(1, f)]
            parts = []
            for d in range(f):
                which = (digit - d) % f
                if f == 2:
                    parts.append(jnp.where(which == 0, got[0], got[1]))
                else:
                    parts.append(lax.select_n(which, *got))
            place = sum(1 for a in done if a < axis)
            dims = tuple(self.factors[a] for a in sorted(done))
            tail = shard.shape
            parts = [p.reshape(dims + tail) for p in parts]
            cur = jnp.stack(parts, axis=place)
            done.append(axis)
            cur = cur.reshape((-1,) + tail)
        return cur.reshape((-1, shard.shape[1]))

    def scatter(self, whole, color):
        cols = whole.shape[1]
        left = list(range(len(self.factors)))
        cur = whole.reshape(self.factors + (-1, cols))
        order = list(reversed(self.orders()[color]))
        for n, axis in enumerate(order):
            f = self.factors[axis]
            digit = self.digits[axis]
            place = left.index(axis)

            def part(at):
                return lax.dynamic_index_in_dim(cur, at, place, keepdims=False)

            got = [self.shift(part((digit + s) % f), axis, s) for s in range(1, f)]
            total = part(digit).astype(f32)
            for g in got:
                total = total + g.astype(f32)
            cur = total if n == len(order) - 1 else total.astype(bf16)
            left.remove(axis)
        return cur

    def total(self, value):
        step = 1
        while step < self.count:
            value = value + lax.ppermute(
                value, "dp", [(i, i ^ step) for i in range(self.count)])
            step *= 2
        return value


def shards(
    tokens_in,
    grad_out,
    doc_len,
    doc_pad,
    doc_owner,
    doc_perm,
    w_query,
    key_matrix,
    value_matrix,
    w_output,
    w_gate,
    w_up,
    w_down,
    gain_attn,
    gain_mlp,
    gain_query,
    gain_key,
):
    devices = lax.axis_size("dp")
    my_index = lax.axis_index("dp")
    core = lax.axis_index("tensor")
    moves = Moves(devices, my_index)
    tables = layout_tables(doc_len, doc_pad, doc_owner, doc_perm, TILE, devices)
    owner_tiles = tables[4]
    owner_start = tables[5]
    home_tiles = tokens_in.shape[0] // TILE
    slot_tiles = CAP_T // devices
    rows_total = CAP_T * TILE
    owners = jnp.arange(devices, dtype=jnp.int32)
    slot_index = jnp.arange(slot_tiles, dtype=jnp.int32)
    is_mine = owners == my_index
    run_start = jnp.sum(jnp.where(is_mine, owner_start, 0))
    run_tiles = jnp.sum(jnp.where(is_mine, owner_tiles, 0))
    residue = (my_index - owner_start) % devices
    target = devices * slot_index[None, :] + residue[:, None]
    sending = target < owner_tiles[:, None]
    source_tile = jnp.where(
        sending, (owner_start[:, None] + target - my_index) // devices, 0
    ).reshape(-1)

    def pack(rows):
        width = rows.shape[1]
        tiles = rows.reshape(home_tiles, TILE, width)
        picked = jnp.take(tiles, source_tile, axis=0).reshape(devices, slot_tiles, TILE, width)
        picked = jnp.where(sending[:, :, None, None], picked, jnp.zeros((), rows.dtype))
        return picked.reshape(devices, slot_tiles * TILE, width)

    buffer_tile = jnp.arange(CAP_T, dtype=jnp.int32)
    source_device = (buffer_tile % devices + run_start) % devices
    arrive_index = source_device * slot_tiles + buffer_tile // devices

    def unpack(received):
        width = received.shape[2]
        tiles = received.reshape(devices * slot_tiles, TILE, width)
        return jnp.take(tiles, arrive_index, axis=0).reshape(rows_total, width)

    back_target = devices * slot_index[None, :] + ((owners - run_start) % devices)[:, None]
    back_valid = back_target < run_tiles
    back_index = jnp.where(back_valid, back_target, 0).reshape(-1)

    def pack_back(rows):
        width = rows.shape[1]
        tiles = rows.reshape(CAP_T, TILE, width)
        picked = jnp.take(tiles, back_index, axis=0).reshape(devices, slot_tiles, TILE, width)
        picked = jnp.where(back_valid[:, :, None, None], picked, jnp.zeros((), rows.dtype))
        return picked.reshape(devices, slot_tiles * TILE, width)

    home_packed = jnp.arange(home_tiles, dtype=jnp.int32) * devices + my_index
    owned = (home_packed[:, None] >= owner_start[None, :]) & (
        home_packed[:, None] < (owner_start + owner_tiles)[None, :]
    )
    owner_of = jnp.sum(jnp.where(owned, owners[None, :], 0), axis=1)
    start_of = jnp.sum(jnp.where(owned, owner_start[None, :], 0), axis=1)
    home_index = owner_of * slot_tiles + (home_packed - start_of) // devices

    def unpack_home(received):
        width = received.shape[2]
        tiles = received.reshape(devices * slot_tiles, TILE, width)
        return jnp.take(tiles, home_index, axis=0).reshape(home_tiles * TILE, width)

    def exchange(value):
        return lax.ppermute(value, "tensor", [(0, 1), (1, 0)])

    def both_halves(own):
        other = exchange(own)
        return jnp.concatenate(
            [jnp.where(core == 0, own, other), jnp.where(core == 0, other, own)], axis=1
        )

    def to_owner(v):
        return lax.all_to_all(v, "dp", split_axis=0, concat_axis=0, tiled=True)

    own_tokens = unpack(to_owner(pack(tokens_in)))
    own_grads = unpack(to_owner(pack(grad_out)))
    position, valid = buffer_rows(my_index, tables, CAP_T, TILE)
    cot_half = jnp.where(valid[:, None], own_grads, jnp.zeros((), bf16))
    half_width = own_tokens.shape[1]

    wq = moves.gather(w_query, 0)
    wkv = moves.gather(jnp.concatenate([key_matrix, value_matrix], axis=1), 1)
    out_rows = jnp.transpose(w_output)
    out_half = out_rows.shape[1] // 2
    wo0 = moves.gather(out_rows[:, :out_half], 0)
    wo1 = moves.gather(out_rows[:, out_half:], 1)
    wg = moves.gather(w_gate, 0)
    wu = moves.gather(w_up, 1)
    down_rows = jnp.transpose(w_down)
    down_half = down_rows.shape[1] // 2
    wd0 = moves.gather(down_rows[:, :down_half], 0)
    wd1 = moves.gather(down_rows[:, down_half:], 1)

    row_index = jnp.arange(rows_total, dtype=jnp.int32)
    start = jnp.where(valid, row_index - position, row_index)
    blocks = rows_total // BLK
    by_block = start.reshape(blocks, BLK)
    lo = by_block[:, 0] // BLK
    hm = jnp.minimum((by_block[:, -1] + BLK - 1) // BLK, jnp.arange(blocks, dtype=jnp.int32))
    start_col = start[:, None]
    start_row = start[None, :]
    cosine, sine = rope_tables(position, HEAD_DIM)
    gq = gain_query[None, :]
    gk = gain_key[None, :]
    g_attn = gain_attn[None, :]
    g_mlp = gain_mlp[None, :]

    x = both_halves(own_tokens)
    normed, q, k, v, raw = qkv_call(x, wq, wkv, g_attn, gq, gk, cosine, sine)
    pairs = k.shape[1] // HEAD_DIM // 2
    att0, il0 = attend_call(lo, hm, q, k, v, start_col, 0, pairs)
    att1, il1 = attend_call(lo, hm, q, k, v, start_col, pairs, pairs)
    attn_part = (dot(att0, wo0, 1, 1) + dot(att1, wo1, 1, 1)).astype(bf16)
    mid, normed2, gate, up, act0, act1, branch = mlp_call(
        x, attn_part, exchange(attn_part), g_mlp, wg, wu, wd0, wd1)

    def half_of(v, which):
        return lax.dynamic_slice_in_dim(v, which * half_width, half_width, 1)

    def half_sum(v):
        return half_of(v, core).astype(f32) + exchange(half_of(v, 1 - core)).astype(f32)

    tokens_out_own = (half_of(mid, core) + half_sum(branch)).astype(bf16)
    cot = both_halves(cot_half)
    grads = {}
    grads["d0"] = moves.scatter(dot(cot, act0, 0, 0).astype(bf16), 0)
    grads["d1"] = moves.scatter(dot(cot, act1, 0, 0).astype(bf16), 1)
    d_gate, d_up, d_mid_part, gain_mlp_part = mlp_back_call(
        cot, mid, gate, up, g_mlp, wg, wu, wd0, wd1)
    grads["g"] = moves.scatter(dot(normed2, d_gate, 0, 0).astype(bf16), 0)
    grads["u"] = moves.scatter(dot(normed2, d_up, 0, 0).astype(bf16), 1)
    d_mid = cot.astype(f32) + (d_mid_part.astype(f32) + exchange(d_mid_part).astype(f32))
    d_mid_low = d_mid.astype(bf16)
    d_att0 = dot(d_mid_low, wo0, 1, 0).astype(bf16)
    d_att1 = dot(d_mid_low, wo1, 1, 0).astype(bf16)
    grads["o0"] = moves.scatter(dot(d_mid_low, att0, 0, 0).astype(bf16), 0)
    grads["o1"] = moves.scatter(dot(d_mid_low, att1, 0, 0).astype(bf16), 1)
    dq0, dk0, dv0, gains0 = attend_back_call(
        lo, hm, q, k, v, att0, d_att0, il0, start_row, raw, cosine, sine, gq, gk, 0, pairs)
    dq1, dk1, dv1, gains1 = attend_back_call(
        lo, hm, q, k, v, att1, d_att1, il1, start_row, raw, cosine, sine, gq, gk, pairs, pairs)
    d_x_part, gain_attn_part = in_back_call(dq0, dq1, dk0, dk1, dv0, dv1, x, g_attn, wq, wkv)

    def grad_a(parts, color):
        return moves.scatter(
            jnp.concatenate([dot(normed, p, 0, 0).astype(bf16) for p in parts], axis=1), color)

    grad_head0 = grad_a((dq0, dk0, dv0), 0)
    grad_head1 = grad_a((dq1, dk1, dv1), 1)
    grad_in_own = (half_of(d_mid, core) + half_sum(d_x_part)).astype(bf16)

    gains = jnp.concatenate(
        [gain_attn_part, gain_mlp_part, gains0[0:1] + gains1[0:1], gains0[1:2] + gains1[1:2]], axis=1)
    gains = moves.total(gains + exchange(gains))[0]
    width = x.shape[1]
    hq = dq0.shape[1]
    hk = dk0.shape[1]

    out_grads = (
        jnp.concatenate([grad_head0[:, :hq], grad_head1[:, :hq]], axis=1),
        jnp.concatenate([grad_head0[:, hq:hq + hk], grad_head1[:, hq:hq + hk]], axis=1),
        jnp.concatenate([grad_head0[:, hq + hk:], grad_head1[:, hq + hk:]], axis=1),
        jnp.transpose(jnp.concatenate([grads["o0"], grads["o1"]], axis=1)),
        grads["g"],
        grads["u"],
        jnp.transpose(jnp.concatenate([grads["d0"], grads["d1"]], axis=1)),
    )
    return (
        unpack_home(to_owner(pack_back(tokens_out_own))),
        unpack_home(to_owner(pack_back(grad_in_own))),
        *out_grads,
        gains[:width],
        gains[width:2 * width],
        gains[2 * width:2 * width + HEAD_DIM],
        gains[2 * width + HEAD_DIM:],
    )


def solution(mesh):
    in_specs = (
        P("dp", "tensor"),
        P("dp", "tensor"),
        P(),
        P(),
        P(),
        P(),
        P("dp", "tensor"),
        P("dp", "tensor"),
        P("dp", "tensor"),
        P("tensor", "dp"),
        P("dp", "tensor"),
        P("dp", "tensor"),
        P("tensor", "dp"),
        P(),
        P(),
        P(),
        P(),
    )
    out_specs = (
        P("dp", "tensor"),
        P("dp", "tensor"),
        P("dp", "tensor"),
        P("dp", "tensor"),
        P("dp", "tensor"),
        P("tensor", "dp"),
        P("dp", "tensor"),
        P("dp", "tensor"),
        P("tensor", "dp"),
        P(),
        P(),
        P(),
        P(),
    )
    return jax.shard_map(shards, mesh=mesh, in_specs=in_specs, out_specs=out_specs, check_vma=False)
```
